32 devices in a mesh: tri: 4 (over z), colx: 4 (over x, core), coly: 2 (over y).
Axes of the slice: x: 2, y: 2, z: 4, core: 2. Of those that a mesh axis runs over, the one named last changes fastest.
Arguments:
- weight: float32 [13824, 5120], P(('colx', 'coly'), 'tri'), may hold values from -6 to 6
- tiles: int32 [48, 3], replicated, may hold values from 0 to 19, as said below
Outputs:
- correction: float32 [13824, 5120], P(('colx', 'coly'), 'tri')
- updated: float32 [13824, 5120], P(('colx', 'coly'), 'tri')
The draws below stay inside these ranges and needn't reach their ends.
Inputs may be any that keep to these rules, and one draw needn't show every extreme that they name: `tiles`: each row is (i, j, owner) with i <= j < 20 and owner < 4; no pair is listed twice; one owner has exactly 24 rows and every other owner at most 24; the rows stand in no particular order.
All inputs are finite; a program needn't handle non-finite values.
Results may differ from the reference program's by a relative error of at most 0.0003.
Values sent between devices are 32-bit elements; how exact they have to be, the bound alone decides.
No kernel may reach another device: no remote copies, remote signals or barrier semaphores. Data moves between devices by JAX's collectives and lax.ppermute only.
A program may use at most 192 MiB of HBM per device.

```python
import jax
import jax.numpy as jnp
import numpy as np
from jax import lax

ROWS = 5120
COLS = 13824
PANEL = 256
PANEL_COUNT = 20
TILES = 48
MOST = 24
N_TRI = 4


def draw_tiles(key, part):
    first_panel_array, second_np = np.triu_indices(PANEL_COUNT)
    first_all = jnp.asarray(first_panel_array, jnp.int32)
    second_all = jnp.asarray(second_np, jnp.int32)
    key_pick, key_busy, key_other, key_order = jax.random.split(key, 4)
    picked = jax.random.permutation(key_pick, first_panel_array.shape[0])[:TILES]
    first = first_all[picked]
    second = second_all[picked]
    busiest = jax.random.randint(key_busy, (), 0, N_TRI)
    others = jax.random.randint(key_other, (TILES,), 1, N_TRI)
    owner = jnp.where(jnp.arange(TILES) < MOST, busiest, (busiest + others) % N_TRI)
    order = jax.random.permutation(key_order, TILES)
    table = jnp.stack([first, second, owner.astype(jnp.int32)], axis=1)
    return table[order].astype(jnp.int32)


def steps_of(key, dims, cuts, smallest, largest):
    loudness, own = 1.0, jax.random.fold_in(key, 6)
    for axis_at, blocks in cuts:
        draws = jnp.exp(jax.random.uniform(jax.random.fold_in(own, axis_at), (blocks,), jnp.float32, smallest / len(cuts), largest / len(cuts)))
        loudness = loudness * jnp.repeat(draws, dims[axis_at] // blocks).reshape([-1 if axis == axis_at else 1 for axis in range(len(dims))])
    return loudness


def scatter_about(key, shape, spread, limit, shards=(), kind=jnp.bfloat16):
    result = spread * jax.random.normal(key, shape, jnp.float32)
    if shards:
        result = result * steps_of(key, shape, shards, -0.22, 0.18)
    return jnp.clip(result, -limit, limit).astype(kind)


def setup_inputs(seed: int = 0) -> dict:
    splits = jax.random.split(jax.random.key(seed), 3)
    weight = scatter_about(splits[0], (COLS, ROWS), 1.0, 6.0, ((0, 8), (1, 4)), jnp.float32)
    tiles = draw_tiles(jax.random.fold_in(splits[2], 71), 0)
    return {"weight": weight, "tiles": tiles}


def reference(weight, tiles):
    panels = weight.T.reshape(PANEL_COUNT, PANEL, COLS)
    top_precision = lax.Precision.HIGHEST

    def add_tile(total, row):
        first = row[0].astype(jnp.int32)
        second = row[1].astype(jnp.int32)
        left = lax.dynamic_index_in_dim(panels, first, 0, keepdims=False)
        right = lax.dynamic_index_in_dim(panels, second, 0, keepdims=False)
        gram = jnp.dot(left, right.T, precision=top_precision, preferred_element_type=jnp.float32) / COLS
        upper_panel = jnp.dot(gram, right, precision=top_precision, preferred_element_type=jnp.float32)
        lower_panel = jnp.dot(gram.T, left, precision=top_precision, preferred_element_type=jnp.float32)
        lower_panel = lower_panel * (first != second).astype(jnp.float32)
        total = total.at[first].add(upper_panel)
        total = total.at[second].add(lower_panel)
        return total, None

    start = jnp.zeros((PANEL_COUNT, PANEL, COLS), jnp.float32)
    total, unused = lax.scan(add_tile, start, tiles)
    correction = total.reshape(ROWS, COLS).T
    updated = 1.5 * weight - 0.5 * correction
    return correction, updated
```

```python
import functools

import jax
import jax.numpy as jnp
from jax import lax
from jax.experimental import pallas as pl
from jax.experimental.pallas import tpu as pltpu
from jax.sharding import PartitionSpec as P

PANEL = 256
VMEM_LIMIT = 56 * 1024 * 1024
GROUP = 4


def split(x):
    high = x.astype(jnp.bfloat16)
    low = (x - high.astype(jnp.float32)).astype(jnp.bfloat16)
    return high, low


def product(left, right, dims):
    (lh, ll), (rh, rl) = left, right

    def dot(a, b):
        return lax.dot_general(a, b, (dims, ((), ())), preferred_element_type=jnp.float32)

    return dot(lh, rh) + (dot(lh, rl) + dot(ll, rh))


def gram_kernel(scale, n, per, where, *refs):
    pieces = refs[:n]
    gram, high, low, turned_high, turned_low = refs[n:]
    step = pl.program_id(0)

    @pl.when(step == 0)
    def _():
        for d in range(n):
            for s in range(per):
                x = pieces[d][:, s * PANEL : (s + 1) * PANEL]
                h, l = split(x)
                high[d * per + s] = h
                low[d * per + s] = l
                h, l = split(x.T)
                turned_high[d * per + s] = h
                turned_low[d * per + s] = l

    for t in range(GROUP):
        k = step * GROUP + t
        i, j = where[k, 0], where[k, 1]
        gram[t] = scale * product(
            (turned_high[i], turned_low[i]), (high[j], low[j]), ((1,), (0,))
        )


def gram_call(where, pieces, scale):
    n = len(pieces)
    rows, width = pieces[0].shape
    per = width // PANEL
    count = where.shape[0]
    whole = pl.BlockSpec((rows, width), lambda k, w: (0, 0), pipeline_mode=pl.Buffered(1))
    kept = pl.BlockSpec((n * per, rows, PANEL), lambda k, w: (0, 0, 0), pipeline_mode=pl.Buffered(1))
    return pl.pallas_call(
        functools.partial(gram_kernel, scale, n, per),
        grid_spec=pltpu.PrefetchScalarGridSpec(
            num_scalar_prefetch=1,
            grid=(count // GROUP,),
            in_specs=[whole] * n,
            out_specs=[pl.BlockSpec((GROUP, PANEL, PANEL), lambda k, w: (k, 0, 0)), kept, kept],
            scratch_shapes=[pltpu.VMEM((n * per, PANEL, rows), jnp.bfloat16)] * 2,
        ),
        out_shape=[
            jax.ShapeDtypeStruct((count, PANEL, PANEL), jnp.float32),
            jax.ShapeDtypeStruct((n * per, rows, PANEL), jnp.bfloat16),
            jax.ShapeDtypeStruct((n * per, rows, PANEL), jnp.bfloat16),
        ],
        compiler_params=pltpu.CompilerParams(
            dimension_semantics=("arbitrary",), vmem_limit_bytes=VMEM_LIMIT
        ),
        cost_estimate=pl.CostEstimate(
            flops=6 * count * PANEL * PANEL * rows,
            bytes_accessed=8 * n * rows * width + 4 * count * PANEL * PANEL,
            transcendentals=0,
        ),
        name="gram",
    )(where, *pieces)


BLOCK = 8


def correction_kernel(table, gram, high, low, out):
    step = pl.program_id(0)

    @pl.when(step == 0)
    def _():
        out[...] = jnp.zeros_like(out)

    def one(t, carry):
        k = step * BLOCK + t
        i, j, first, second = table[k, 0], table[k, 1], table[k, 2], table[k, 3]

        @pl.when(first >= 0)
        def _():
            at = pl.ds(pl.multiple_of(first * PANEL, PANEL), PANEL)
            out[:, at] += product((high[j], low[j]), split(gram[t]), ((1,), (1,)))

        @pl.when(second >= 0)
        def _():
            at = pl.ds(pl.multiple_of(second * PANEL, PANEL), PANEL)
            out[:, at] += product((high[i], low[i]), split(gram[t]), ((1,), (0,)))

        return carry

    lax.fori_loop(0, BLOCK, one, 0)


def correction_call(table, gram, high, low, per):
    slots, rows, _ = high.shape
    count = table.shape[0]
    kept = pl.BlockSpec((slots, rows, PANEL), lambda k, w: (0, 0, 0), pipeline_mode=pl.Buffered(1))
    return pl.pallas_call(
        correction_kernel,
        grid_spec=pltpu.PrefetchScalarGridSpec(
            num_scalar_prefetch=1,
            grid=(count // BLOCK,),
            in_specs=[pl.BlockSpec((BLOCK, PANEL, PANEL), lambda k, w: (k, 0, 0)), kept, kept],
            out_specs=pl.BlockSpec((rows, per * PANEL), lambda k, w: (0, 0), pipeline_mode=pl.Buffered(1)),
        ),
        out_shape=jax.ShapeDtypeStruct((rows, per * PANEL), jnp.float32),
        compiler_params=pltpu.CompilerParams(
            dimension_semantics=("arbitrary",), vmem_limit_bytes=VMEM_LIMIT
        ),
        cost_estimate=pl.CostEstimate(
            flops=3 * count * PANEL * PANEL * rows,
            bytes_accessed=4 * slots * rows * PANEL + 4 * count * PANEL * PANEL,
            transcendentals=0,
        ),
        name="correction",
    )(table, gram, high, low)


def on_device(columns, weight, tiles):
    n = lax.axis_size("tri")
    z = lax.axis_index("tri")
    local, width = weight.shape
    per = width // PANEL
    rows = -(-local // (n * 16)) * 16
    padded = jnp.pad(weight, ((0, n * rows - local), (0, 0))) if n * rows != local else weight

    def ring(d):
        return [(s, (s + d) % n) for s in range(n)]

    def chunk(d):
        return lax.dynamic_slice_in_dim(padded, lax.rem(z + d, n) * rows, rows, 0)

    pieces = [None] * n
    order = sorted(range(1, n), key=lambda d: abs(d - n // 2))
    for d in order:
        pieces[d] = lax.ppermute(chunk(d), "tri", ring(d))
    pieces[0] = chunk(0)

    first, second = tiles[:, 0], tiles[:, 1]

    def place(panel):
        return lax.rem(z - panel // per + n, n) * per + panel % per

    where = jnp.stack([place(first), place(second)], axis=1)
    gram, high, low = gram_call(where, pieces, 1.0 / columns)
    gram = lax.psum(gram, ("tri", "colx", "coly"))

    def target(panel, d):
        return jnp.where(panel // per == lax.rem(z + d, n), panel % per, -1)

    results = [None] * n
    for d in order + [0]:
        onto = jnp.where(first == second, -1, target(second, d))
        table = jnp.stack([place(first), place(second), target(first, d), onto], axis=1)
        part = correction_call(table, gram, high, low, per)
        results[d] = lax.ppermute(part, "tri", ring(d)) if d else part

    correction = jnp.zeros_like(padded)
    updated = padded
    for d in [0] + order:
        at = lax.rem(z - d + n, n) * rows
        old = lax.dynamic_slice_in_dim(padded, at, rows, 0)
        correction = lax.dynamic_update_slice_in_dim(correction, results[d], at, 0)
        updated = lax.dynamic_update_slice_in_dim(updated, 1.5 * old - 0.5 * results[d], at, 0)
    return correction[:local], updated[:local]


def solution(mesh):
    spec = P(("colx", "coly"), "tri")

    def step(weight, tiles):
        body = jax.shard_map(
            functools.partial(on_device, weight.shape[0]),
            mesh=mesh,
            in_specs=(spec, P()),
            out_specs=(spec, spec),
            check_vma=False,
        )
        return body(weight, tiles)

    return step
```

```python
import functools
import math

import jax
import jax.numpy as jnp
from jax import lax
from jax.experimental import pallas as pl
from jax.experimental.pallas import tpu as pltpu
from jax.sharding import PartitionSpec as P


PANEL = 256
VMEM_LIMIT = 56 * 1024 * 1024
GROUP = 4


def split(x):
    high = x.astype(jnp.bfloat16)
    low = (x - high.astype(jnp.float32)).astype(jnp.bfloat16)
    return high, low


def product(left, right, dims):
    (lh, ll), (rh, rl) = left, right

    def dot(a, b):
        return lax.dot_general(a, b, (dims, ((), ())), preferred_element_type=jnp.float32)

    return dot(lh, rh) + (dot(lh, rl) + dot(ll, rh))


def load_kernel(n, per, *refs):
    pieces = refs[:n]
    high, low, turned_high, turned_low = refs[n:]
    for d in range(n):
        for s in range(per):
            x = pieces[d][:, s * PANEL : (s + 1) * PANEL]
            high[d * per + s], low[d * per + s] = split(x)
            turned_high[d * per + s], turned_low[d * per + s] = split(x.T)


def gram_first_kernel(scale, n, per, where, *refs):
    pieces = refs[:n]
    gram, kept = refs[n], refs[n + 1 :]

    @pl.when(pl.program_id(0) == 0)
    def _():
        load_kernel(n, per, *pieces, *kept)

    gram_kernel(scale, where, *kept, gram)


def gram_kernel(scale, where, high, low, turned_high, turned_low, gram):
    for t in range(GROUP):
        k = pl.program_id(0) * GROUP + t
        i, j = where[k, 0], where[k, 1]
        gram[t] = scale * product((turned_high[i], turned_low[i]), (high[j], low[j]), ((1,), (0,)))


def still(shape):
    return pl.BlockSpec(shape, lambda k, w: (0,) * len(shape), pipeline_mode=pl.Buffered(1))


def gram_call(where, arrays, scale, first):
    count = where.shape[0]
    n = len(arrays)
    if first:
        rows, width = arrays[0].shape
        slots = n * width // PANEL
    else:
        slots, rows, _ = arrays[0].shape
    kept = [(slots, rows, PANEL)] * 2 + [(slots, PANEL, rows)] * 2
    gram_spec = pl.BlockSpec((GROUP, PANEL, PANEL), lambda k, w: (k, 0, 0))
    gram_shape = jax.ShapeDtypeStruct((count, PANEL, PANEL), jnp.float32)
    return pl.pallas_call(
        functools.partial(gram_first_kernel, scale, n, slots // n)
        if first
        else functools.partial(gram_kernel, scale),
        grid_spec=pltpu.PrefetchScalarGridSpec(
            num_scalar_prefetch=1,
            grid=(count // GROUP,),
            in_specs=[still(a.shape) for a in arrays],
            out_specs=[gram_spec] + [still(shape) for shape in kept] if first else gram_spec,
        ),
        out_shape=[gram_shape] + [jax.ShapeDtypeStruct(shape, jnp.bfloat16) for shape in kept]
        if first
        else gram_shape,
        compiler_params=pltpu.CompilerParams(
            dimension_semantics=("arbitrary",), vmem_limit_bytes=VMEM_LIMIT
        ),
        cost_estimate=pl.CostEstimate(
            flops=6 * count * PANEL * PANEL * rows,
            bytes_accessed=8 * slots * rows * PANEL + 4 * count * PANEL * PANEL,
            transcendentals=0,
        ),
        name="gram_first" if first else "gram",
    )(where, *arrays)


def correction_kernel(parts, raw, table, *refs):
    grams = refs[:parts]
    step = pl.program_id(0)
    if raw:
        out, high, low = refs[parts + raw :]

        @pl.when(step == 0)
        def _():
            per = high.shape[0] // raw
            for d in range(raw):
                for s in range(per):
                    x = refs[parts + d][:, s * PANEL : (s + 1) * PANEL]
                    high[d * per + s], low[d * per + s] = split(x)

    else:
        high, low, out = refs[parts:]
    size = grams[0].shape[0]
    steps = pl.num_programs(0)

    @pl.when(step == 0)
    def _():
        out[...] = jnp.zeros_like(out)

    for part in range(parts):
        gram = grams[part]

        def one(t, carry):
            k = (part * steps + step) * size + t
            i, j, first, second = table[k, 0], table[k, 1], table[k, 2], table[k, 3]

            @pl.when(first >= 0)
            def _():
                at = pl.ds(pl.multiple_of(first * PANEL, PANEL), PANEL)
                out[:, at] += product((high[j], low[j]), split(gram[t]), ((1,), (1,)))

            @pl.when(second >= 0)
            def _():
                at = pl.ds(pl.multiple_of(second * PANEL, PANEL), PANEL)
                out[:, at] += product((high[i], low[i]), split(gram[t]), ((1,), (0,)))

            return carry

        lax.fori_loop(0, size, one, 0)


BLOCK = 2


def correction_call(table, grams, arrays, rows, per):
    raw = arrays[0].ndim == 2
    if raw:
        slots = len(arrays) * per
        specs, scratch = [still(a.shape) for a in arrays], [pltpu.VMEM((slots, rows, PANEL), jnp.bfloat16)] * 2
    else:
        slots = arrays[0].shape[0]
        specs, scratch = [still((slots, rows, PANEL))] * 2, []
    count = grams[0].shape[0]
    return pl.pallas_call(
        functools.partial(correction_kernel, len(grams), len(arrays) if raw else 0),
        grid_spec=pltpu.PrefetchScalarGridSpec(
            num_scalar_prefetch=1,
            grid=(count // BLOCK,),
            in_specs=[pl.BlockSpec((BLOCK, PANEL, PANEL), lambda k, w: (k, 0, 0))] * len(grams)
            + specs,
            out_specs=still((rows, per * PANEL)),
            scratch_shapes=scratch,
        ),
        out_shape=jax.ShapeDtypeStruct((rows, per * PANEL), jnp.float32),
        compiler_params=pltpu.CompilerParams(
            dimension_semantics=("arbitrary",), vmem_limit_bytes=VMEM_LIMIT
        ),
        cost_estimate=pl.CostEstimate(
            flops=3 * table.shape[0] * PANEL * PANEL * rows,
            bytes_accessed=4 * slots * rows * PANEL + 4 * table.shape[0] * PANEL * PANEL,
            transcendentals=0,
        ),
        name="correction",
    )(table, *grams, *arrays)


def place_kernel(at, part, weight, *refs):
    correction, updated = refs[-2:]
    correction[...] = part[...]
    updated[...] = 1.5 * weight[...] - 0.5 * part[...]


def place_call(at, part, weight, earlier, block):
    size, width = part.shape
    here = pl.BlockSpec((block, width), lambda g, a: (g, 0))
    there = pl.BlockSpec((block, width), lambda g, a: (a[0] + g, 0))
    return pl.pallas_call(
        place_kernel,
        grid_spec=pltpu.PrefetchScalarGridSpec(
            num_scalar_prefetch=1,
            grid=(size // block,),
            in_specs=[here, there] + [pl.BlockSpec(memory_space=pl.ANY)] * len(earlier),
            out_specs=[there, there],
        ),
        out_shape=[jax.ShapeDtypeStruct(weight.shape, weight.dtype)] * 2,
        input_output_aliases={3: 0, 4: 1} if earlier else {},
        compiler_params=pltpu.CompilerParams(dimension_semantics=("arbitrary",)),
        cost_estimate=pl.CostEstimate(flops=3 * size * width, bytes_accessed=16 * size * width, transcendentals=0),
        name="place",
    )(at[None] // block, part, weight, *earlier)


together = lax.optimization_barrier


def flip(value, dim):
    axis, mask = dim
    pairs = [(s, s ^ mask) for s in range(lax.axis_size(axis))]
    return lax.ppermute(value, axis, pairs)


def side(dim):
    axis, mask = dim
    return lax.axis_index(axis) // mask % 2


def bits_of(axis, lowest=1):
    size, mask, found = lax.axis_size(axis), lowest, []
    while mask < size:
        found.append((axis, mask))
        mask *= 2
    return found[::-1]


def cut(terms, start, rows):
    return sum(lax.dynamic_slice_in_dim(t, base + start, rows, 0) for base, t in terms)


def whole_sum(kept, got, orders):
    colours, rows = len(orders), kept.shape[0] // len(orders)
    terms = [[(c * rows, t) for t in (kept, got)] for c in range(colours)]
    for dims in zip(*orders):
        rows //= 2
        sides = [side(dim) for dim in dims]
        sent = together([cut(t, (1 - b) * rows, rows) for t, b in zip(terms, sides)])
        came = [flip(v, dim) for v, dim in zip(sent, dims)]
        mine = [cut(t, b * rows, rows) for t, b in zip(terms, sides)]
        terms = [[(0, a), (0, b)] for a, b in zip(mine, together(came))]
    done = together([a + b for (_, a), (_, b) in terms])
    for dims in list(zip(*orders))[:0:-1]:
        came = together([flip(v, dim) for v, dim in zip(done, dims)])
        joined = []
        for v, w, dim in zip(done, came, dims):
            if rows % PANEL:
                b = side(dim)
                both = lax.dynamic_update_slice_in_dim(jnp.zeros_like(jnp.concatenate([v, w])), v, b * rows, 0)
                joined.append(lax.dynamic_update_slice_in_dim(both, w, (1 - b) * rows, 0))
            else:
                joined.append(jnp.concatenate([v, w]))
        rows *= 2
        done = together(joined)
    came = [flip(v, dim) for v, dim in zip(done, [order[0] for order in orders])]
    return done, came


def tile_at(orders, core, count):
    places = jnp.arange(count, dtype=jnp.int32)
    per = count // 2 // len(orders)
    buffer, place = places // (count // 4), places % (count // 4)
    colour, spot = place // (per // 2), place % (per // 2)
    half = jnp.stack([side(order[0]) for order in orders])[colour]
    tile = half ^ (buffer % 2)
    unit, level = per // 2, 1
    while unit % 2 == 0:
        unit //= 2
        other = jnp.stack([side(order[level]) for order in orders])[colour]
        tile = tile * 2 + (spot // unit % 2 ^ other)
        level += 1
    tile = tile * unit + spot % unit
    return (core ^ (buffer // 2)) * (count // 2) + colour * per + tile


def on_device(columns, weight, tiles):
    n = lax.axis_size("tri")
    z = lax.axis_index("tri")
    local, width = weight.shape
    per = width // PANEL
    count = tiles.shape[0]
    rows = -(-local // (n * 16)) * 16
    padded = jnp.pad(weight, ((0, n * rows - local), (0, 0))) if n * rows != local else weight

    core_dim = ("colx", 1)
    along_x, along_y, along_z = bits_of("colx", 2), bits_of("coly"), bits_of("tri")
    near, far = along_z[1:], along_z[:1]
    orders = [along_x + along_y + near + far, along_y + near + along_x + far, near + along_x + along_y + far]
    core = side(core_dim)

    def place(panel):
        return (z ^ (panel // per)) * per + panel % per

    def target(panel, d):
        return jnp.where(panel // per == z ^ d, panel % per, -1)

    first, second = tiles[:, 0], tiles[:, 1]
    where = jnp.stack([place(first), place(second)], axis=1)
    half = count // 2
    where_sent = lax.dynamic_slice_in_dim(where, (1 - core) * half, half, 0)
    where_kept = lax.dynamic_slice_in_dim(where, core * half, half, 0)
    stood = tiles[tile_at(orders, core, count)]
    first, second = stood[:, 0], stood[:, 1]
    tables = []
    for d in range(n):
        onto = jnp.where(first == second, -1, target(second, d))
        tables.append(jnp.stack([place(first), place(second), target(first, d), onto], axis=1))

    order = list(range(n - 1, 0, -1))
    pieces = [None] * n
    source = padded
    for d in order:
        chunk = lax.dynamic_slice_in_dim(source, (z ^ d) * rows, rows, 0)
        source, chunk = together((source, chunk))
        pieces[d] = flip(chunk, ("tri", d))
    pieces[0] = lax.dynamic_slice_in_dim(source, z * rows, rows, 0)

    top = n // 2
    more = rows // 3 // 16 * 16
    less = rows - more
    mirrored = []
    if more:
        for d in range(n):
            chunk = lax.dynamic_slice_in_dim(source, (z ^ d ^ top) * rows + less, more, 0)
            source, chunk = together((source, chunk))
            mirrored.append(chunk)
        pieces, mirrored = together((pieces, mirrored))
        mirrored = [flip(chunk, ("tri", d)) if d else chunk for d, chunk in enumerate(mirrored)]

    sent, *panels = gram_call(where_sent, pieces, 1.0 / columns, True)
    got = flip(sent, core_dim)

    kept = gram_call(where_kept, panels, 1.0 / columns, False)
    here, there = whole_sum(kept.reshape(half * PANEL, PANEL), got.reshape(half * PANEL, PANEL), orders)
    here = jnp.concatenate(here)
    here_other = flip(here, core_dim)
    there = jnp.concatenate(there)
    there_other = flip(there, core_dim)
    grams = [g.reshape(count // 4, PANEL, PANEL) for g in (here, there, here_other, there_other)]

    ready = []
    for d in range(n - 1, -1, -1):
        found = [((z ^ d) * rows, correction_call(tables[d], grams, panels[:2], less if d >= top else rows, per))]
        if more and d < top:
            found.append(((z ^ d ^ top) * rows + less, correction_call(tables[d], grams, mirrored, more, per)))
        if d:
            ready += [(at, flip(part, ("tri", d))) for at, part in found]
        else:
            ready = found + ready

    block = math.gcd(rows, more)
    placed = ()
    for at, part in ready:
        placed = place_call(at, part, padded, placed, block)
    correction, updated = placed
    return correction[:local], updated[:local]


def solution(mesh):
    spec = P(("colx", "coly"), "tri")

    def step(weight, tiles):
        body = jax.shard_map(
            functools.partial(on_device, weight.shape[0]),
            mesh=mesh,
            in_specs=(spec, P()),
            out_specs=(spec, spec),
            check_vma=False,
        )
        return body(weight, tiles)

    return step
```

```python
import functools
import math

import jax
import jax.numpy as jnp
from jax import lax
from jax.experimental import pallas as pl
from jax.experimental.pallas import tpu as pltpu
from jax.sharding import PartitionSpec as P


PANEL = 256
VMEM_LIMIT = 56 * 1024 * 1024
GROUP = 4


def split(x):
    high = x.astype(jnp.bfloat16)
    low = (x - high.astype(jnp.float32)).astype(jnp.bfloat16)
    return high, low


def product(left, right, dims):
    (lh, ll), (rh, rl) = left, right

    def dot(a, b):
        return lax.dot_general(a, b, (dims, ((), ())), preferred_element_type=jnp.float32)

    return dot(lh, rh) + (dot(lh, rl) + dot(ll, rh))


def load_kernel(n, per, *refs):
    pieces = refs[:n]
    high, low = refs[n:]
    for d in range(n):
        for s in range(per):
            high[d * per + s], low[d * per + s] = split(pieces[d][:, s * PANEL : (s + 1) * PANEL])


def gram_first_kernel(scale, n, per, where, *refs):
    pieces = refs[:n]
    gram, kept = refs[n], refs[n + 1 :]

    @pl.when(pl.program_id(0) == 0)
    def _():
        load_kernel(n, per, *pieces, *kept)

    gram_kernel(scale, where, *kept, gram)


def gram_kernel(scale, where, high, low, gram):
    for t in range(GROUP):
        k = pl.program_id(0) * GROUP + t
        i, j = where[k, 0], where[k, 1]
        gram[t] = scale * product((high[i], low[i]), (high[j], low[j]), ((0,), (0,)))


def still(shape):
    return pl.BlockSpec(shape, lambda k, w: (0,) * len(shape), pipeline_mode=pl.Buffered(1))


def gram_call(where, arrays, scale, first):
    count = where.shape[0]
    n = len(arrays)
    if first:
        rows, width = arrays[0].shape
        slots = n * width // PANEL
    else:
        slots, rows, _ = arrays[0].shape
    kept = [(slots, rows, PANEL)] * 2
    gram_spec = pl.BlockSpec((GROUP, PANEL, PANEL), lambda k, w: (k, 0, 0))
    gram_shape = jax.ShapeDtypeStruct((count, PANEL, PANEL), jnp.float32)
    return pl.pallas_call(
        functools.partial(gram_first_kernel, scale, n, slots // n)
        if first
        else functools.partial(gram_kernel, scale),
        grid_spec=pltpu.PrefetchScalarGridSpec(
            num_scalar_prefetch=1,
            grid=(count // GROUP,),
            in_specs=[still(a.shape) for a in arrays],
            out_specs=[gram_spec] + [still(shape) for shape in kept] if first else gram_spec,
        ),
        out_shape=[gram_shape] + [jax.ShapeDtypeStruct(shape, jnp.bfloat16) for shape in kept]
        if first
        else gram_shape,
        compiler_params=pltpu.CompilerParams(
            dimension_semantics=("arbitrary",), vmem_limit_bytes=VMEM_LIMIT
        ),
        cost_estimate=pl.CostEstimate(
            flops=6 * count * PANEL * PANEL * rows,
            bytes_accessed=8 * slots * rows * PANEL + 4 * count * PANEL * PANEL,
            transcendentals=0,
        ),
        name="gram_first" if first else "gram",
    )(where, *arrays)


def correction_kernel(parts, raw, table, *refs):
    grams = refs[:parts]
    step = pl.program_id(0)
    if raw:
        out, high, low = refs[parts + raw :]

        @pl.when(step == 0)
        def _():
            per = high.shape[0] // raw
            for d in range(raw):
                for s in range(per):
                    x = refs[parts + d][:, s * PANEL : (s + 1) * PANEL]
                    high[d * per + s], low[d * per + s] = split(x)

    else:
        high, low, out = refs[parts:]
    size = grams[0].shape[0]
    steps = pl.num_programs(0)

    @pl.when(step == 0)
    def _():
        out[...] = jnp.zeros_like(out)

    for part in range(parts):
        gram = grams[part]

        def one(t, carry):
            k = (part * steps + step) * size + t
            i, j, first, second = table[k, 0], table[k, 1], table[k, 2], table[k, 3]

            @pl.when(first >= 0)
            def _():
                at = pl.ds(pl.multiple_of(first * PANEL, PANEL), PANEL)
                out[:, at] += product((high[j], low[j]), split(gram[t]), ((1,), (1,)))

            @pl.when(second >= 0)
            def _():
                at = pl.ds(pl.multiple_of(second * PANEL, PANEL), PANEL)
                out[:, at] += product((high[i], low[i]), split(gram[t]), ((1,), (0,)))

            return carry

        lax.fori_loop(0, size, one, 0)


BLOCK = 2


def correction_call(table, grams, arrays, rows, per):
    raw = arrays[0].ndim == 2
    if raw:
        slots = len(arrays) * per
        specs, scratch = [still(a.shape) for a in arrays], [pltpu.VMEM((slots, rows, PANEL), jnp.bfloat16)] * 2
    else:
        slots = arrays[0].shape[0]
        specs, scratch = [still((slots, rows, PANEL))] * 2, []
    count = grams[0].shape[0]
    return pl.pallas_call(
        functools.partial(correction_kernel, len(grams), len(arrays) if raw else 0),
        grid_spec=pltpu.PrefetchScalarGridSpec(
            num_scalar_prefetch=1,
            grid=(count // BLOCK,),
            in_specs=[pl.BlockSpec((BLOCK, PANEL, PANEL), lambda k, w: (k, 0, 0))] * len(grams)
            + specs,
            out_specs=still((rows, per * PANEL)),
            scratch_shapes=scratch,
        ),
        out_shape=jax.ShapeDtypeStruct((rows, per * PANEL), jnp.float32),
        compiler_params=pltpu.CompilerParams(
            dimension_semantics=("arbitrary",), vmem_limit_bytes=VMEM_LIMIT
        ),
        cost_estimate=pl.CostEstimate(
            flops=3 * table.shape[0] * PANEL * PANEL * rows,
            bytes_accessed=4 * slots * rows * PANEL + 4 * table.shape[0] * PANEL * PANEL,
            transcendentals=0,
        ),
        name="correction",
    )(table, *grams, *arrays)


def place_kernel(at, part, weight, *refs):
    correction, updated = refs[-2:]
    correction[...] = part[...]
    updated[...] = 1.5 * weight[...] - 0.5 * part[...]


def place_call(at, part, weight, earlier, block):
    size, width = part.shape
    here = pl.BlockSpec((block, width), lambda g, a: (g, 0))
    there = pl.BlockSpec((block, width), lambda g, a: (a[0] + g, 0))
    return pl.pallas_call(
        place_kernel,
        grid_spec=pltpu.PrefetchScalarGridSpec(
            num_scalar_prefetch=1,
            grid=(size // block,),
            in_specs=[here, there] + [pl.BlockSpec(memory_space=pl.ANY)] * len(earlier),
            out_specs=[there, there],
        ),
        out_shape=[jax.ShapeDtypeStruct(weight.shape, weight.dtype)] * 2,
        input_output_aliases={3: 0, 4: 1} if earlier else {},
        compiler_params=pltpu.CompilerParams(dimension_semantics=("arbitrary",)),
        cost_estimate=pl.CostEstimate(flops=3 * size * width, bytes_accessed=16 * size * width, transcendentals=0),
        name="place",
    )(at[None] // block, part, weight, *earlier)


def eager_kernel(parts, per, table, *refs):
    grams = refs[:parts]
    high, low, out, held, high_here, low_here, gram_sem, side_sem = refs[parts:]
    slots, rows, _ = high_here.shape
    size = grams[0].shape[0]

    def sides(g):
        part = pl.ds(g * per, per)
        return [
            pltpu.make_async_copy(far.at[part, pl.ds(0, rows)], near.at[part], side_sem.at[which, g])
            for which, (far, near) in enumerate(((high, high_here), (low, low_here)))
        ]

    for g in range(slots // per):
        for copy in sides(g):
            copy.start()

    def each(do):
        for part in range(parts):

            def one(t, carry):
                k = part * size + t
                first, second = table[k, 2], table[k, 3]

                @pl.when(jnp.maximum(first, second) >= 0)
                def _():
                    do(k, pltpu.make_async_copy(grams[part].at[t], held.at[k], gram_sem.at[k]))

                return carry

            lax.fori_loop(0, size, one, 0)

    each(lambda k, copy: copy.start())
    out[...] = jnp.zeros_like(out)
    for g in range(slots // per):
        for copy in sides(g):
            copy.wait()

    def add(k, copy):
        copy.wait()
        i, j, first, second = table[k, 0], table[k, 1], table[k, 2], table[k, 3]

        @pl.when(first >= 0)
        def _():
            at = pl.ds(pl.multiple_of(first * PANEL, PANEL), PANEL)
            out[:, at] += product((high_here[j], low_here[j]), split(held[k]), ((1,), (1,)))

        @pl.when(second >= 0)
        def _():
            at = pl.ds(pl.multiple_of(second * PANEL, PANEL), PANEL)
            out[:, at] += product((high_here[i], low_here[i]), split(held[k]), ((1,), (0,)))

    each(add)


def eager_call(table, grams, arrays, rows, per):
    slots, count = arrays[0].shape[0], table.shape[0]
    return pl.pallas_call(
        functools.partial(eager_kernel, len(grams), per),
        grid_spec=pltpu.PrefetchScalarGridSpec(
            num_scalar_prefetch=1,
            grid=(1,),
            in_specs=[pl.BlockSpec(memory_space=pl.ANY)] * (len(grams) + 2),
            out_specs=still((rows, per * PANEL)),
            scratch_shapes=[
                pltpu.VMEM((count, PANEL, PANEL), jnp.float32),
                pltpu.VMEM((slots, rows, PANEL), jnp.bfloat16),
                pltpu.VMEM((slots, rows, PANEL), jnp.bfloat16),
                pltpu.SemaphoreType.DMA((count,)),
                pltpu.SemaphoreType.DMA((2, slots // per)),
            ],
        ),
        out_shape=jax.ShapeDtypeStruct((rows, per * PANEL), jnp.float32),
        compiler_params=pltpu.CompilerParams(
            dimension_semantics=("arbitrary",), vmem_limit_bytes=VMEM_LIMIT
        ),
        cost_estimate=pl.CostEstimate(
            flops=3 * count * PANEL * PANEL * rows,
            bytes_accessed=4 * slots * rows * PANEL + 4 * count * PANEL * PANEL,
            transcendentals=0,
        ),
        name="eager",
    )(table, *grams, *arrays)


together = lax.optimization_barrier


def flip(value, dim):
    axis, mask = dim
    pairs = [(s, s ^ mask) for s in range(lax.axis_size(axis))]
    return lax.ppermute(value, axis, pairs)


def side(dim):
    axis, mask = dim
    return lax.axis_index(axis) // mask % 2


def bits_of(axis, lowest=1):
    size, mask, found = lax.axis_size(axis), lowest, []
    while mask < size:
        found.append((axis, mask))
        mask *= 2
    return found[::-1]


def cut(terms, start, rows):
    return sum(lax.dynamic_slice_in_dim(t, base + start, rows, 0) for base, t in terms)


def whole_sum(kept, got, orders):
    colours, rows = len(orders), kept.shape[0] // len(orders)
    terms = [[(c * rows, t) for t in (kept, got)] for c in range(colours)]
    for dims in zip(*orders):
        rows //= 2
        sides = [side(dim) for dim in dims]
        sent = together([cut(t, (1 - b) * rows, rows) for t, b in zip(terms, sides)])
        came = [flip(v, dim) for v, dim in zip(sent, dims)]
        mine = [cut(t, b * rows, rows) for t, b in zip(terms, sides)]
        terms = [[(0, a), (0, b)] for a, b in zip(mine, together(came))]
    done = together([a + b for (_, a), (_, b) in terms])
    for dims in list(zip(*orders))[:0:-1]:
        came = together([flip(v, dim) for v, dim in zip(done, dims)])
        joined = []
        for v, w, dim in zip(done, came, dims):
            if rows % PANEL:
                b = side(dim)
                both = lax.dynamic_update_slice_in_dim(jnp.zeros_like(jnp.concatenate([v, w])), v, b * rows, 0)
                joined.append(lax.dynamic_update_slice_in_dim(both, w, (1 - b) * rows, 0))
            else:
                joined.append(jnp.concatenate([v, w]))
        rows *= 2
        done = together(joined)
    came = [flip(v, dim) for v, dim in zip(done, [order[0] for order in orders])]
    return done, came


def tile_at(orders, core, count):
    places = jnp.arange(count, dtype=jnp.int32)
    per = count // 2 // len(orders)
    buffer, place = places // (count // 4), places % (count // 4)
    colour, spot = place // (per // 2), place % (per // 2)
    half = jnp.stack([side(order[0]) for order in orders])[colour]
    tile = half ^ (buffer % 2)
    unit, level = per // 2, 1
    while unit % 2 == 0:
        unit //= 2
        other = jnp.stack([side(order[level]) for order in orders])[colour]
        tile = tile * 2 + (spot // unit % 2 ^ other)
        level += 1
    tile = tile * unit + spot % unit
    return (core ^ (buffer // 2)) * (count // 2) + colour * per + tile


def on_device(columns, weight, tiles):
    n = lax.axis_size("tri")
    z = lax.axis_index("tri")
    local, width = weight.shape
    per = width // PANEL
    count = tiles.shape[0]
    rows = -(-local // (n * 16)) * 16
    padded = jnp.pad(weight, ((0, n * rows - local), (0, 0))) if n * rows != local else weight

    core_dim = ("colx", 1)
    along_x, along_y, along_z = bits_of("colx", 2), bits_of("coly"), bits_of("tri")
    near, far = along_z[1:], along_z[:1]
    orders = [along_x + along_y + near + far, along_y + near + along_x + far, near + along_x + along_y + far]
    core = side(core_dim)

    def place(panel):
        return (z ^ (panel // per)) * per + panel % per

    def target(panel, d):
        return jnp.where(panel // per == z ^ d, panel % per, -1)

    first, second = tiles[:, 0], tiles[:, 1]
    where = jnp.stack([place(first), place(second)], axis=1)
    half = count // 2
    where_sent = lax.dynamic_slice_in_dim(where, (1 - core) * half, half, 0)
    where_kept = lax.dynamic_slice_in_dim(where, core * half, half, 0)
    stood = tiles[tile_at(orders, core, count)]
    first, second = stood[:, 0], stood[:, 1]
    tables = []
    for d in range(n):
        onto = jnp.where(first == second, -1, target(second, d))
        tables.append(jnp.stack([place(first), place(second), target(first, d), onto], axis=1))

    order = list(range(n - 1, 0, -1))
    pieces = [None] * n
    source = padded
    for d in order:
        chunk = lax.dynamic_slice_in_dim(source, (z ^ d) * rows, rows, 0)
        source, chunk = together((source, chunk))
        pieces[d] = flip(chunk, ("tri", d))
    pieces[0] = lax.dynamic_slice_in_dim(source, z * rows, rows, 0)

    top = n // 2
    more = rows // 3 // 16 * 16
    less = rows - more
    mirrored = []
    if more:
        for d in range(n):
            chunk = lax.dynamic_slice_in_dim(source, (z ^ d ^ top) * rows + less, more, 0)
            source, chunk = together((source, chunk))
            mirrored.append(chunk)
        pieces, mirrored = together((pieces, mirrored))
        mirrored = [flip(chunk, ("tri", d)) if d else chunk for d, chunk in enumerate(mirrored)]

    sent, *panels = gram_call(where_sent, pieces, 1.0 / columns, True)
    got = flip(sent, core_dim)

    kept = gram_call(where_kept, panels, 1.0 / columns, False)
    here, there = whole_sum(kept.reshape(half * PANEL, PANEL), got.reshape(half * PANEL, PANEL), orders)
    here = jnp.concatenate(here)
    here_other = flip(here, core_dim)
    there = jnp.concatenate(there)
    there_other = flip(there, core_dim)
    grams = [g.reshape(count // 4, PANEL, PANEL) for g in (here, there, here_other, there_other)]

    ready = [[], [], [], []]
    for d in range(n - 1, -1, -1):
        found = [((z ^ d) * rows, eager_call(tables[d], grams, panels, less if d >= top else rows, per))]
        if more and d < top:
            found.append(((z ^ d ^ top) * rows + less, correction_call(tables[d], grams, mirrored, more, per)))
        when = 0 if d == 0 else 1 if d > top else 3 if d == top else 2
        ready[when] += [(at, flip(part, ("tri", d)) if d else part) for at, part in found]
    ready = sum(ready, [])

    block = math.gcd(rows, more)
    placed = ()
    for at, part in ready:
        placed = place_call(at, part, padded, placed, block)
    correction, updated = placed
    return correction[:local], updated[:local]


def solution(mesh):
    spec = P(("colx", "coly"), "tri")

    def step(weight, tiles):
        body = jax.shard_map(
            functools.partial(on_device, weight.shape[0]),
            mesh=mesh,
            in_specs=(spec, P()),
            out_specs=(spec, spec),
            check_vma=False,
        )
        return body(weight, tiles)

    return step
```

```python
import functools
import math

import jax
import jax.numpy as jnp
from jax import lax
from jax.experimental import pallas as pl
from jax.experimental.pallas import tpu as pltpu
from jax.sharding import PartitionSpec as P


PANEL = 256
VMEM_LIMIT = 56 * 1024 * 1024
GROUP = 4


def split(x):
    high = x.astype(jnp.bfloat16)
    low = (x - high.astype(jnp.float32)).astype(jnp.bfloat16)
    return high, low


def product(left, right, dims):
    (lh, ll), (rh, rl) = left, right

    def dot(a, b):
        return lax.dot_general(a, b, (dims, ((), ())), preferred_element_type=jnp.float32)

    return dot(lh, rh) + (dot(lh, rl) + dot(ll, rh))


def load_kernel(n, per, *refs):
    pieces = refs[:n]
    high, low = refs[n:]
    for d in range(n):
        for s in range(per):
            high[d * per + s], low[d * per + s] = split(pieces[d][:, s * PANEL : (s + 1) * PANEL])


def gram_first_kernel(scale, n, per, where, *refs):
    pieces = refs[:n]
    gram, kept = refs[n], refs[n + 1 :]

    @pl.when(pl.program_id(0) == 0)
    def _():
        load_kernel(n, per, *pieces, *kept)

    gram_kernel(scale, where, *kept, gram)


def gram_kernel(scale, where, high, low, gram):
    for t in range(GROUP):
        k = pl.program_id(0) * GROUP + t
        i, j = where[k, 0], where[k, 1]
        gram[t] = scale * product((high[i], low[i]), (high[j], low[j]), ((0,), (0,)))


def still(shape):
    return pl.BlockSpec(shape, lambda k, w: (0,) * len(shape), pipeline_mode=pl.Buffered(1))


def gram_call(where, arrays, scale, first):
    count = where.shape[0]
    n = len(arrays)
    if first:
        rows, width = arrays[0].shape
        slots = n * width // PANEL
    else:
        slots, rows, _ = arrays[0].shape
    kept = [(slots, rows, PANEL)] * 2
    gram_spec = pl.BlockSpec((GROUP, PANEL, PANEL), lambda k, w: (k, 0, 0))
    gram_shape = jax.ShapeDtypeStruct((count, PANEL, PANEL), jnp.float32)
    return pl.pallas_call(
        functools.partial(gram_first_kernel, scale, n, slots // n)
        if first
        else functools.partial(gram_kernel, scale),
        grid_spec=pltpu.PrefetchScalarGridSpec(
            num_scalar_prefetch=1,
            grid=(count // GROUP,),
            in_specs=[still(a.shape) for a in arrays],
            out_specs=[gram_spec] + [still(shape) for shape in kept] if first else gram_spec,
        ),
        out_shape=[gram_shape] + [jax.ShapeDtypeStruct(shape, jnp.bfloat16) for shape in kept]
        if first
        else gram_shape,
        compiler_params=pltpu.CompilerParams(
            dimension_semantics=("arbitrary",), vmem_limit_bytes=VMEM_LIMIT
        ),
        cost_estimate=pl.CostEstimate(
            flops=6 * count * PANEL * PANEL * rows,
            bytes_accessed=8 * slots * rows * PANEL + 4 * count * PANEL * PANEL,
            transcendentals=0,
        ),
        name="gram_first" if first else "gram",
    )(where, *arrays)


def correction_kernel(parts, raw, table, *refs):
    grams = refs[:parts]
    step = pl.program_id(0)
    if raw:
        out, high, low = refs[parts + raw :]

        @pl.when(step == 0)
        def _():
            per = high.shape[0] // raw
            for d in range(raw):
                for s in range(per):
                    x = refs[parts + d][:, s * PANEL : (s + 1) * PANEL]
                    high[d * per + s], low[d * per + s] = split(x)

    else:
        high, low, out = refs[parts:]
    size = grams[0].shape[0]
    steps = pl.num_programs(0)

    @pl.when(step == 0)
    def _():
        out[...] = jnp.zeros_like(out)

    for part in range(parts):
        gram = grams[part]

        def one(t, carry):
            k = (part * steps + step) * size + t
            i, j, first, second = table[k, 0], table[k, 1], table[k, 2], table[k, 3]

            @pl.when(first >= 0)
            def _():
                at = pl.ds(pl.multiple_of(first * PANEL, PANEL), PANEL)
                out[:, at] += product((high[j], low[j]), split(gram[t]), ((1,), (1,)))

            @pl.when(second >= 0)
            def _():
                at = pl.ds(pl.multiple_of(second * PANEL, PANEL), PANEL)
                out[:, at] += product((high[i], low[i]), split(gram[t]), ((1,), (0,)))

            return carry

        lax.fori_loop(0, size, one, 0)


BLOCK = 2


def correction_call(table, grams, arrays, rows, per):
    raw = arrays[0].ndim == 2
    if raw:
        slots = len(arrays) * per
        specs, scratch = [still(a.shape) for a in arrays], [pltpu.VMEM((slots, rows, PANEL), jnp.bfloat16)] * 2
    else:
        slots = arrays[0].shape[0]
        specs, scratch = [still((slots, rows, PANEL))] * 2, []
    count = grams[0].shape[0]
    return pl.pallas_call(
        functools.partial(correction_kernel, len(grams), len(arrays) if raw else 0),
        grid_spec=pltpu.PrefetchScalarGridSpec(
            num_scalar_prefetch=1,
            grid=(count // BLOCK,),
            in_specs=[pl.BlockSpec((BLOCK, PANEL, PANEL), lambda k, w: (k, 0, 0))] * len(grams)
            + specs,
            out_specs=still((rows, per * PANEL)),
            scratch_shapes=scratch,
        ),
        out_shape=jax.ShapeDtypeStruct((rows, per * PANEL), jnp.float32),
        compiler_params=pltpu.CompilerParams(
            dimension_semantics=("arbitrary",), vmem_limit_bytes=VMEM_LIMIT
        ),
        cost_estimate=pl.CostEstimate(
            flops=3 * table.shape[0] * PANEL * PANEL * rows,
            bytes_accessed=4 * slots * rows * PANEL + 4 * table.shape[0] * PANEL * PANEL,
            transcendentals=0,
        ),
        name="correction",
    )(table, *grams, *arrays)


def place_kernel(at, part, weight, *refs):
    correction, updated = refs[-2:]
    correction[...] = part[...]
    updated[...] = 1.5 * weight[...] - 0.5 * part[...]


def place_call(at, part, weight, earlier, block):
    size, width = part.shape
    here = pl.BlockSpec((block, width), lambda g, a: (g, 0))
    there = pl.BlockSpec((block, width), lambda g, a: (a[0] + g, 0))
    return pl.pallas_call(
        place_kernel,
        grid_spec=pltpu.PrefetchScalarGridSpec(
            num_scalar_prefetch=1,
            grid=(size // block,),
            in_specs=[here, there] + [pl.BlockSpec(memory_space=pl.ANY)] * len(earlier),
            out_specs=[there, there],
        ),
        out_shape=[jax.ShapeDtypeStruct(weight.shape, weight.dtype)] * 2,
        input_output_aliases={3: 0, 4: 1} if earlier else {},
        compiler_params=pltpu.CompilerParams(dimension_semantics=("arbitrary",)),
        cost_estimate=pl.CostEstimate(flops=3 * size * width, bytes_accessed=16 * size * width, transcendentals=0),
        name="place",
    )(at[None] // block, part, weight, *earlier)


def eager_kernel(parts, per, begin, table, *refs):
    grams = refs[:parts]
    high, low, out, held, high_here, low_here, gram_sem, side_sem = refs[parts:]
    slots, rows, _ = high_here.shape
    size = grams[0].shape[0]

    def sides(g):
        part = pl.ds(g * per, per)
        return [
            pltpu.make_async_copy(far.at[part, pl.ds(begin, rows)], near.at[part], side_sem.at[which, g])
            for which, (far, near) in enumerate(((high, high_here), (low, low_here)))
        ]

    for g in range(slots // per):
        for copy in sides(g):
            copy.start()

    def each(do):
        for part in range(parts):

            def one(t, carry):
                k = part * size + t
                first, second = table[k, 2], table[k, 3]

                @pl.when(jnp.maximum(first, second) >= 0)
                def _():
                    do(k, pltpu.make_async_copy(grams[part].at[t], held.at[k], gram_sem.at[k]))

                return carry

            lax.fori_loop(0, size, one, 0)

    each(lambda k, copy: copy.start())
    out[...] = jnp.zeros_like(out)
    for g in range(slots // per):
        for copy in sides(g):
            copy.wait()

    def add(k, copy):
        copy.wait()
        i, j, first, second = table[k, 0], table[k, 1], table[k, 2], table[k, 3]

        @pl.when(first >= 0)
        def _():
            at = pl.ds(pl.multiple_of(first * PANEL, PANEL), PANEL)
            out[:, at] += product((high_here[j], low_here[j]), split(held[k]), ((1,), (1,)))

        @pl.when(second >= 0)
        def _():
            at = pl.ds(pl.multiple_of(second * PANEL, PANEL), PANEL)
            out[:, at] += product((high_here[i], low_here[i]), split(held[k]), ((1,), (0,)))

    each(add)


def eager_call(table, grams, arrays, begin, rows, per):
    slots, count = arrays[0].shape[0], table.shape[0]
    return pl.pallas_call(
        functools.partial(eager_kernel, len(grams), per, begin),
        grid_spec=pltpu.PrefetchScalarGridSpec(
            num_scalar_prefetch=1,
            grid=(1,),
            in_specs=[pl.BlockSpec(memory_space=pl.ANY)] * (len(grams) + 2),
            out_specs=still((rows, per * PANEL)),
            scratch_shapes=[
                pltpu.VMEM((count, PANEL, PANEL), jnp.float32),
                pltpu.VMEM((slots, rows, PANEL), jnp.bfloat16),
                pltpu.VMEM((slots, rows, PANEL), jnp.bfloat16),
                pltpu.SemaphoreType.DMA((count,)),
                pltpu.SemaphoreType.DMA((2, slots // per)),
            ],
        ),
        out_shape=jax.ShapeDtypeStruct((rows, per * PANEL), jnp.float32),
        compiler_params=pltpu.CompilerParams(
            dimension_semantics=("arbitrary",), vmem_limit_bytes=VMEM_LIMIT
        ),
        cost_estimate=pl.CostEstimate(
            flops=3 * count * PANEL * PANEL * rows,
            bytes_accessed=4 * slots * rows * PANEL + 4 * count * PANEL * PANEL,
            transcendentals=0,
        ),
        name="eager",
    )(table, *grams, *arrays)


together = lax.optimization_barrier


def flip(value, dim):
    axis, mask = dim
    pairs = [(s, s ^ mask) for s in range(lax.axis_size(axis))]
    return lax.ppermute(value, axis, pairs)


def side(dim):
    axis, mask = dim
    return lax.axis_index(axis) // mask % 2


def bits_of(axis, lowest=1):
    size, mask, found = lax.axis_size(axis), lowest, []
    while mask < size:
        found.append((axis, mask))
        mask *= 2
    return found[::-1]


def cut(terms, start, rows):
    return sum(lax.dynamic_slice_in_dim(t, base + start, rows, 0) for base, t in terms)


def whole_sum(kept, got, orders):
    colours, rows = len(orders), kept.shape[0] // len(orders)
    terms = [[(c * rows, t) for t in (kept, got)] for c in range(colours)]
    for dims in zip(*orders):
        rows //= 2
        sides = [side(dim) for dim in dims]
        sent = together([cut(t, (1 - b) * rows, rows) for t, b in zip(terms, sides)])
        came = [flip(v, dim) for v, dim in zip(sent, dims)]
        mine = [cut(t, b * rows, rows) for t, b in zip(terms, sides)]
        terms = [[(0, a), (0, b)] for a, b in zip(mine, together(came))]
    done = together([a + b for (_, a), (_, b) in terms])
    for dims in list(zip(*orders))[:0:-1]:
        came = together([flip(v, dim) for v, dim in zip(done, dims)])
        joined = []
        for v, w, dim in zip(done, came, dims):
            if rows % PANEL:
                b = side(dim)
                both = lax.dynamic_update_slice_in_dim(jnp.zeros_like(jnp.concatenate([v, w])), v, b * rows, 0)
                joined.append(lax.dynamic_update_slice_in_dim(both, w, (1 - b) * rows, 0))
            else:
                joined.append(jnp.concatenate([v, w]))
        rows *= 2
        done = together(joined)
    came = [flip(v, dim) for v, dim in zip(done, [order[0] for order in orders])]
    return done, came


def tile_at(orders, core, count):
    places = jnp.arange(count, dtype=jnp.int32)
    per = count // 2 // len(orders)
    buffer, place = places // (count // 4), places % (count // 4)
    colour, spot = place // (per // 2), place % (per // 2)
    half = jnp.stack([side(order[0]) for order in orders])[colour]
    tile = half ^ (buffer % 2)
    unit, level = per // 2, 1
    while unit % 2 == 0:
        unit //= 2
        other = jnp.stack([side(order[level]) for order in orders])[colour]
        tile = tile * 2 + (spot // unit % 2 ^ other)
        level += 1
    tile = tile * unit + spot % unit
    return (core ^ (buffer // 2)) * (count // 2) + colour * per + tile


def on_device(columns, weight, tiles):
    n = lax.axis_size("tri")
    z = lax.axis_index("tri")
    local, width = weight.shape
    per = width // PANEL
    count = tiles.shape[0]
    rows = -(-local // (n * 16)) * 16
    padded = jnp.pad(weight, ((0, n * rows - local), (0, 0))) if n * rows != local else weight

    core_dim = ("colx", 1)
    along_x, along_y, along_z = bits_of("colx", 2), bits_of("coly"), bits_of("tri")
    near, far = along_z[1:], along_z[:1]
    orders = [along_x + along_y + near + far, along_y + near + along_x + far, near + along_x + along_y + far]
    core = side(core_dim)

    def place(panel):
        return (z ^ (panel // per)) * per + panel % per

    def target(panel, d):
        return jnp.where(panel // per == z ^ d, panel % per, -1)

    first, second = tiles[:, 0], tiles[:, 1]
    where = jnp.stack([place(first), place(second)], axis=1)
    half = count // 2
    where_sent = lax.dynamic_slice_in_dim(where, (1 - core) * half, half, 0)
    where_kept = lax.dynamic_slice_in_dim(where, core * half, half, 0)
    stood = tiles[tile_at(orders, core, count)]
    first, second = stood[:, 0], stood[:, 1]
    tables = []
    for d in range(n):
        onto = jnp.where(first == second, -1, target(second, d))
        tables.append(jnp.stack([place(first), place(second), target(first, d), onto], axis=1))

    order = list(range(n - 1, 0, -1))
    pieces = [None] * n
    source = padded
    for d in order:
        chunk = lax.dynamic_slice_in_dim(source, (z ^ d) * rows, rows, 0)
        source, chunk = together((source, chunk))
        pieces[d] = flip(chunk, ("tri", d))
    pieces[0] = lax.dynamic_slice_in_dim(source, z * rows, rows, 0)

    top = n // 2
    more = rows // 3 // 16 * 16
    less = rows - more
    mirrored = []
    if more:
        for d in range(n):
            chunk = lax.dynamic_slice_in_dim(source, (z ^ d ^ top) * rows + less, more, 0)
            source, chunk = together((source, chunk))
            if 0 < d < top:
                chunk = flip(chunk, ("tri", d))
            mirrored.append(chunk)
        pieces, mirrored = together((pieces, mirrored))
        mirrored = mirrored[:top] + [flip(mirrored[d], ("tri", d)) for d in range(top, n)]

    sent, *panels = gram_call(where_sent, pieces, 1.0 / columns, True)
    got = flip(sent, core_dim)

    kept = gram_call(where_kept, panels, 1.0 / columns, False)
    here, there = whole_sum(kept.reshape(half * PANEL, PANEL), got.reshape(half * PANEL, PANEL), orders)
    here = jnp.concatenate(here)
    here_other = flip(here, core_dim)
    there = jnp.concatenate(there)
    there_other = flip(there, core_dim)
    grams = [g.reshape(count // 4, PANEL, PANEL) for g in (here, there, here_other, there_other)]

    ready = [[], [], [], []]
    part, turn = grams[0], 0
    for d in range(n - 1, -1, -1):
        size = less if d >= top else rows
        jobs = [(eager_call, (panels, 0, size), z ^ d, 0, size)]
        if more and d < top:
            jobs.append((correction_call, (mirrored, more), z ^ d ^ top, less, more))
        when = 0 if d == 0 else 1 if d > top else 3 if d == top else 2
        for call, how, chunk, start, size in jobs:
            table, _ = together((tables[d], part))
            part = call(table, grams, *how, per)
            sent = flip(part, ("tri", d)) if d else part
            turn += 1
            block = math.gcd(rows, math.gcd(start, size))
            block = block // 3 if block == rows and rows % 24 == 0 else block
            ready[when].append((chunk * rows + start, sent, block))

    placed = ()
    for at, part, block in sum(ready, []):
        placed = place_call(at, part, padded, placed, block)
    correction, updated = placed
    return correction[:local], updated[:local]


def solution(mesh):
    spec = P(("colx", "coly"), "tri")

    def step(weight, tiles):
        body = jax.shard_map(
            functools.partial(on_device, weight.shape[0]),
            mesh=mesh,
            in_specs=(spec, P()),
            out_specs=(spec, spec),
            check_vma=False,
        )
        return body(weight, tiles)

    return step
```

```python
import functools
import math

import jax
import jax.numpy as jnp
from jax import lax
from jax.experimental import pallas as pl
from jax.experimental.pallas import tpu as pltpu
from jax.sharding import PartitionSpec as P


PANEL = 256
VMEM_LIMIT = 56 * 1024 * 1024
GROUP = 8


def split(x):
    high = x.astype(jnp.bfloat16)
    low = (x - high.astype(jnp.float32)).astype(jnp.bfloat16)
    return high, low


def product(left, right, dims):
    (lh, ll), (rh, rl) = left, right

    def dot(a, b):
        return lax.dot_general(a, b, (dims, ((), ())), preferred_element_type=jnp.float32)

    return dot(lh, rh) + (dot(lh, rl) + dot(ll, rh))


def load_kernel(n, per, *refs):
    pieces = refs[:n]
    high, low = refs[n:]
    for d in range(n):
        for s in range(per):
            high[d * per + s], low[d * per + s] = split(pieces[d][:, s * PANEL : (s + 1) * PANEL])


def gram_first_kernel(scale, n, per, where, *refs):
    pieces = refs[:n]
    gram, kept = refs[n], refs[n + 1 :]

    @pl.when(pl.program_id(0) == 0)
    def _():
        load_kernel(n, per, *pieces, *kept)

    gram_kernel(scale, where, *kept, gram)


def gram_kernel(scale, where, high, low, gram):
    for t in range(GROUP):
        k = pl.program_id(0) * GROUP + t
        i, j = where[k, 0], where[k, 1]
        gram[t] = scale * product((high[i], low[i]), (high[j], low[j]), ((0,), (0,)))


def still(shape):
    return pl.BlockSpec(shape, lambda k, w: (0,) * len(shape), pipeline_mode=pl.Buffered(1))


def gram_call(where, arrays, scale, first):
    count = where.shape[0]
    n = len(arrays)
    if first:
        rows, width = arrays[0].shape
        slots = n * width // PANEL
    else:
        slots, rows, _ = arrays[0].shape
    kept = [(slots, rows, PANEL)] * 2
    gram_spec = pl.BlockSpec((GROUP, PANEL, PANEL), lambda k, w: (k, 0, 0))
    gram_shape = jax.ShapeDtypeStruct((count, PANEL, PANEL), jnp.float32)
    return pl.pallas_call(
        functools.partial(gram_first_kernel, scale, n, slots // n)
        if first
        else functools.partial(gram_kernel, scale),
        grid_spec=pltpu.PrefetchScalarGridSpec(
            num_scalar_prefetch=1,
            grid=(count // GROUP,),
            in_specs=[still(a.shape) for a in arrays],
            out_specs=[gram_spec] + [still(shape) for shape in kept] if first else gram_spec,
        ),
        out_shape=[gram_shape] + [jax.ShapeDtypeStruct(shape, jnp.bfloat16) for shape in kept]
        if first
        else gram_shape,
        compiler_params=pltpu.CompilerParams(
            dimension_semantics=("arbitrary",), vmem_limit_bytes=VMEM_LIMIT
        ),
        cost_estimate=pl.CostEstimate(
            flops=6 * count * PANEL * PANEL * rows,
            bytes_accessed=8 * slots * rows * PANEL + 4 * count * PANEL * PANEL,
            transcendentals=0,
        ),
        name="gram_first" if first else "gram",
    )(where, *arrays)


def place_kernel(at, part, weight, *refs):
    correction, updated = refs[-2:]
    correction[...] = part[...]
    updated[...] = 1.5 * weight[...] - 0.5 * part[...]


def place_call(at, part, weight, earlier, block):
    size, width = part.shape
    here = pl.BlockSpec((block, width), lambda g, a: (g, 0))
    there = pl.BlockSpec((block, width), lambda g, a: (a[0] + g, 0))
    return pl.pallas_call(
        place_kernel,
        grid_spec=pltpu.PrefetchScalarGridSpec(
            num_scalar_prefetch=1,
            grid=(size // block,),
            in_specs=[here, there] + [pl.BlockSpec(memory_space=pl.ANY)] * len(earlier),
            out_specs=[there, there],
        ),
        out_shape=[jax.ShapeDtypeStruct(weight.shape, weight.dtype)] * 2,
        input_output_aliases={3: 0, 4: 1} if earlier else {},
        compiler_params=pltpu.CompilerParams(dimension_semantics=("arbitrary",)),
        cost_estimate=pl.CostEstimate(flops=3 * size * width, bytes_accessed=16 * size * width, transcendentals=0),
        name="place",
    )(at[None] // block, part, weight, *earlier)


def eager_kernel(parts, per, raw, table, *refs):
    grams, refs = refs[:parts], refs[parts:]
    sources, (out, held, high_here, low_here, gram_sem, side_sem) = refs[:-6], refs[-6:]
    slots, rows, _ = high_here.shape
    size = grams[0].shape[0]
    count = table.shape[0]

    def needed(k, do):
        @pl.when(jnp.maximum(table[k, 2], table[k, 3]) >= 0)
        def _():
            do()

    def sides(g):
        part = pl.ds(g * per, per)
        return [
            pltpu.make_async_copy(far.at[part, pl.ds(0, rows)], near.at[part], side_sem.at[which, g])
            for which, (far, near) in enumerate(zip(sources, (high_here, low_here)))
        ]

    if not raw:
        for g in range(slots // per):
            for copy in sides(g):
                copy.start()

    for part in range(parts):

        def fetch(t, carry):
            k = part * size + t
            needed(k, lambda: pltpu.make_async_copy(grams[part].at[t], held.at[k], gram_sem.at[k]).start())
            return carry

        lax.fori_loop(0, size, fetch, 0)

    out[...] = jnp.zeros_like(out)
    for g in range(slots // per):
        if raw:
            for s in range(per):
                x = sources[g][:, s * PANEL : (s + 1) * PANEL]
                high_here[g * per + s], low_here[g * per + s] = split(x)
        else:
            for copy in sides(g):
                copy.wait()

    def add(k):
        pltpu.make_async_copy(grams[0].at[0], held.at[k], gram_sem.at[k]).wait()
        i, j, first, second = table[k, 0], table[k, 1], table[k, 2], table[k, 3]

        @pl.when(first >= 0)
        def _():
            at = pl.ds(pl.multiple_of(first * PANEL, PANEL), PANEL)
            out[:, at] += product((high_here[j], low_here[j]), split(held[k]), ((1,), (1,)))

        @pl.when(second >= 0)
        def _():
            at = pl.ds(pl.multiple_of(second * PANEL, PANEL), PANEL)
            out[:, at] += product((high_here[i], low_here[i]), split(held[k]), ((1,), (0,)))

    def one(k, carry):
        needed(k, lambda: add(k))
        return carry

    lax.fori_loop(0, count, one, 0)


def eager_call(table, grams, arrays, rows, per):
    raw = arrays[0].ndim == 2
    count = table.shape[0]
    slots = len(arrays) * per if raw else arrays[0].shape[0]
    anywhere = pl.BlockSpec(memory_space=pl.ANY)
    return pl.pallas_call(
        functools.partial(eager_kernel, len(grams), per, raw),
        grid_spec=pltpu.PrefetchScalarGridSpec(
            num_scalar_prefetch=1,
            grid=(1,),
            in_specs=[anywhere] * len(grams) + [still(a.shape) if raw else anywhere for a in arrays],
            out_specs=still((rows, per * PANEL)),
            scratch_shapes=[
                pltpu.VMEM((count, PANEL, PANEL), jnp.float32),
                pltpu.VMEM((slots, rows, PANEL), jnp.bfloat16),
                pltpu.VMEM((slots, rows, PANEL), jnp.bfloat16),
                pltpu.SemaphoreType.DMA((count,)),
                pltpu.SemaphoreType.DMA((2, slots // per)),
            ],
        ),
        out_shape=jax.ShapeDtypeStruct((rows, per * PANEL), jnp.float32),
        compiler_params=pltpu.CompilerParams(
            dimension_semantics=("arbitrary",), vmem_limit_bytes=VMEM_LIMIT
        ),
        cost_estimate=pl.CostEstimate(
            flops=3 * count * PANEL * PANEL * rows,
            bytes_accessed=4 * slots * rows * PANEL + 4 * count * PANEL * PANEL,
            transcendentals=0,
        ),
        name="eager",
    )(table, *grams, *arrays)


together = lax.optimization_barrier


def flip(value, dim):
    axis, mask = dim
    pairs = [(s, s ^ mask) for s in range(lax.axis_size(axis))]
    return lax.ppermute(value, axis, pairs)


def side(dim):
    axis, mask = dim
    return lax.axis_index(axis) // mask % 2


def bits_of(axis, lowest=1):
    size, mask, found = lax.axis_size(axis), lowest, []
    while mask < size:
        found.append((axis, mask))
        mask *= 2
    return found[::-1]


def cut(terms, start, rows):
    return sum(lax.dynamic_slice_in_dim(t, base + start, rows, 0) for base, t in terms)


def whole_sum(kept, got, orders):
    colours, rows = len(orders), kept.shape[0] // len(orders)
    terms = [[(c * rows, t) for t in (kept, got)] for c in range(colours)]
    for dims in zip(*orders):
        rows //= 2
        sides = [side(dim) for dim in dims]
        sent = together([cut(t, (1 - b) * rows, rows) for t, b in zip(terms, sides)])
        came = [flip(v, dim) for v, dim in zip(sent, dims)]
        mine = [cut(t, b * rows, rows) for t, b in zip(terms, sides)]
        terms = [[(0, a), (0, b)] for a, b in zip(mine, together(came))]
    done = together([a + b for (_, a), (_, b) in terms])
    for dims in list(zip(*orders))[:0:-1]:
        came = together([flip(v, dim) for v, dim in zip(done, dims)])
        joined = []
        for v, w, dim in zip(done, came, dims):
            if rows % PANEL:
                b = side(dim)
                both = lax.dynamic_update_slice_in_dim(jnp.zeros_like(jnp.concatenate([v, w])), v, b * rows, 0)
                joined.append(lax.dynamic_update_slice_in_dim(both, w, (1 - b) * rows, 0))
            else:
                joined.append(jnp.concatenate([v, w]))
        rows *= 2
        done = together(joined)
    came = [flip(v, dim) for v, dim in zip(done, [order[0] for order in orders])]
    return done, came


def tile_at(orders, core, count):
    places = jnp.arange(count, dtype=jnp.int32)
    per = count // 2 // len(orders)
    buffer, place = places // (count // 4), places % (count // 4)
    colour, spot = place // (per // 2), place % (per // 2)
    half = jnp.stack([side(order[0]) for order in orders])[colour]
    tile = half ^ (buffer % 2)
    unit, level = per // 2, 1
    while unit % 2 == 0:
        unit //= 2
        other = jnp.stack([side(order[level]) for order in orders])[colour]
        tile = tile * 2 + (spot // unit % 2 ^ other)
        level += 1
    tile = tile * unit + spot % unit
    return (core ^ (buffer // 2)) * (count // 2) + colour * per + tile


def on_device(columns, weight, tiles):
    n = lax.axis_size("tri")
    z = lax.axis_index("tri")
    local, width = weight.shape
    per = width // PANEL
    count = tiles.shape[0]
    rows = -(-local // (n * 16)) * 16
    padded = jnp.pad(weight, ((0, n * rows - local), (0, 0))) if n * rows != local else weight

    core_dim = ("colx", 1)
    along_x, along_y, along_z = bits_of("colx", 2), bits_of("coly"), bits_of("tri")
    near, far = along_z[1:], along_z[:1]
    orders = [along_x + along_y + near + far, along_y + near + along_x + far, near + along_x + along_y + far]
    core = side(core_dim)

    def place(panel):
        return (z ^ (panel // per)) * per + panel % per

    def target(panel, d):
        return jnp.where(panel // per == z ^ d, panel % per, -1)

    first, second = tiles[:, 0], tiles[:, 1]
    where = jnp.stack([place(first), place(second)], axis=1)
    half = count // 2
    where_sent = lax.dynamic_slice_in_dim(where, (1 - core) * half, half, 0)
    where_kept = lax.dynamic_slice_in_dim(where, core * half, half, 0)
    stood = tiles[tile_at(orders, core, count)]
    first, second = stood[:, 0], stood[:, 1]
    tables = []
    for d in range(n):
        onto = jnp.where(first == second, -1, target(second, d))
        tables.append(jnp.stack([place(first), place(second), target(first, d), onto], axis=1))

    order = list(range(n - 1, 0, -1))
    pieces = [None] * n
    source = padded
    for d in order:
        chunk = lax.dynamic_slice_in_dim(source, (z ^ d) * rows, rows, 0)
        source, chunk = together((source, chunk))
        pieces[d] = flip(chunk, ("tri", d))
    pieces[0] = lax.dynamic_slice_in_dim(source, z * rows, rows, 0)

    top = n // 2
    more = rows // 3 // 16 * 16
    less = rows - more
    mirrored = []
    if more:
        for d in range(n):
            chunk = lax.dynamic_slice_in_dim(source, (z ^ d ^ top) * rows + less, more, 0)
            source, chunk = together((source, chunk))
            if 0 < d < top:
                chunk = flip(chunk, ("tri", d))
            mirrored.append(chunk)
        pieces, mirrored = together((pieces, mirrored))
        mirrored = mirrored[:top] + [flip(mirrored[d], ("tri", d)) for d in range(top, n)]

    sent, *panels = gram_call(where_sent, pieces, 1.0 / columns, True)
    got = flip(sent, core_dim)

    kept = gram_call(where_kept, panels, 1.0 / columns, False)
    here, there = whole_sum(kept.reshape(half * PANEL, PANEL), got.reshape(half * PANEL, PANEL), orders)
    grams = [*here, *there, *[flip(v, core_dim) for v in here], *[flip(v, core_dim) for v in there]]
    grams = [g.reshape(-1, PANEL, PANEL) for g in grams]

    ready = [[], [], [], []]
    part, turn = grams[0], 0
    for d in range(n - 1, -1, -1):
        size = less if d >= top else rows
        jobs = [(panels, z ^ d, 0, size)]
        if more and d < top:
            jobs.append((mirrored, z ^ d ^ top, less, more))
        when = 0 if d == 0 else 1 if d > top else 3 if d == top else 2
        for arrays, chunk, start, size in jobs:
            table, _ = together((tables[d], part))
            part = eager_call(table, grams, arrays, size, per)
            sent = flip(part, ("tri", d)) if d else part
            turn += 1
            block = math.gcd(rows, math.gcd(start, size))
            block = block // 3 if block == rows and rows % 24 == 0 else block
            ready[when].append((chunk * rows + start, sent, block))

    placed = ()
    for at, part, block in sum(ready, []):
        placed = place_call(at, part, padded, placed, block)
    correction, updated = placed
    return correction[:local], updated[:local]


def solution(mesh):
    spec = P(("colx", "coly"), "tri")

    def step(weight, tiles):
        body = jax.shard_map(
            functools.partial(on_device, weight.shape[0]),
            mesh=mesh,
            in_specs=(spec, P()),
            out_specs=(spec, spec),
            check_vma=False,
        )
        return body(weight, tiles)

    return step
```
